32 devices in a mesh: group: 8 (over z, x), fsdp: 4 (over y, core).
Axes of the slice: x: 2, y: 2, z: 4, core: 2. Of those that a mesh axis runs over, the one named last changes fastest.
Arguments:
- mol_qkv: bfloat16 [64, 128, 3, 4096], P('group', None, None, 'fsdp'), may hold values from -12 to 12
- pair_list: int32 [128, 3], replicated, may hold values from 0 to 7, as said below
- head_proj: bfloat16 [32, 128, 256], P('fsdp'), may hold values from -0.5 to 0.5
- head_out: float32 [32, 256], P('fsdp'), may hold values from -0.375 to 0.375
- labels: int32 [128], P('group'), may hold values 0 or 1
Outputs:
- mol_grad: bfloat16 [64, 128, 3, 4096], P('group', None, None, 'fsdp')
- pair_logits: float32 [128], P('group')
- mean_loss: float32 [], replicated
The draws below stay inside these ranges and needn't reach their ends.
Inputs may be any that keep to these rules, and one draw needn't show every extreme that they name: `pair_list`: pair p belongs to owner p // 16; column 0 is the first molecule's index among the owner's 8 molecules, column 1 the group index that holds the second molecule, column 2 its index among that holder's 8 molecules; molecule m is held by group m // 8. `pair_list`: among one owner's pairs, at most 4 take their second molecule from any one holder, and those name at most 2 different molecules; every owner reaches both bounds.
All inputs are finite; a program needn't handle non-finite values. No bound on the sum of `labels` on one device may be relied on, other than what follows from the above.
Results may differ from the reference program's by a relative error of at most 0.0075.
Values may be sent and summed in bfloat16 or wider, within the bound.
A program may use at most 192 MiB of HBM per device.

```python
import jax
import jax.numpy as jnp
from jax import lax

HEADS = 32
HD = 128
R = 256
L = 128
MOL_DEV = 8
MOLS = 64
PAIR_DEV = 16
PAIRS = 128
CAP_PAIR = 4
CAP_MOL = 2


def draw_mol_qkv(key, part):
    keys = jax.random.split(jax.random.fold_in(key, 11), 1)
    shape = (MOLS, L, 3, HEADS * HD)
    values = jax.random.normal(keys[0], shape, jnp.float32)
    return jnp.clip(values, -6.0, 6.0).astype(jnp.bfloat16)


def draw_pair_list(key, part):
    keys = jax.random.split(jax.random.fold_in(key, 23), 7)
    owners = PAIRS // PAIR_DEV
    position = jnp.arange(PAIR_DEV, dtype=jnp.int32)[None, :]
    hub_holder = jax.random.randint(keys[0], (owners, 1), 0, owners)
    offset_base = jax.random.randint(keys[1], (owners, 1), 0, owners - 1)
    other_holder = (hub_holder + 1 + (position - CAP_PAIR + offset_base) % (owners - 1)) % owners
    holder = jnp.where(position < CAP_PAIR, hub_holder, other_holder)
    base_mol = jax.random.randint(keys[2], (owners, 1), 0, MOL_DEV)
    hub_member = (base_mol + position % CAP_MOL) % MOL_DEV
    random_member = jax.random.randint(keys[3], (owners, PAIR_DEV), 0, MOL_DEV)
    member = jnp.where(position < CAP_PAIR, hub_member, random_member)
    first_mol = jnp.minimum(jax.random.randint(keys[4], (owners, PAIR_DEV), 0, MOL_DEV), jax.random.randint(keys[5], (owners, PAIR_DEV), 0, MOL_DEV))
    shuffle_keys = jax.random.randint(keys[6], (owners, PAIR_DEV), 0, 4 * PAIR_DEV) * PAIR_DEV + position
    shuffle = jnp.argsort(shuffle_keys, axis=1, stable=True)
    table = jnp.stack([first_mol, holder, member], axis=2)
    table = jnp.take_along_axis(table, shuffle[:, :, None], axis=1)
    return table.reshape(PAIRS, 3).astype(jnp.int32)


def touch_ends(result, rng, low, high):
    longest = result.shape.index(max(result.shape))
    spots = []
    for shift in (0, 1):
        where = [jax.random.randint(jax.random.fold_in(rng, axis), (), 0, length) for axis, length in enumerate(result.shape)]
        where[longest] = (where[longest] + shift) % result.shape[longest]
        spots.append(tuple(where))
    return result.at[spots[0]].set(low).at[spots[1]].set(high)


def shard_levels(rng, dims, cuts, smallest, largest):
    def one(axis_at, parts):
        draws = jax.random.uniform(jax.random.fold_in(jax.random.fold_in(rng, 6), axis_at), (parts,), jnp.float32, smallest / len(cuts), largest / len(cuts))
        return jnp.repeat(jnp.exp(draws), dims[axis_at] // parts).reshape((-1,) + (1,) * (len(dims) - axis_at - 1))

    loudness = one(*cuts[0])
    for cut in cuts[1:]:
        loudness = loudness * one(*cut)
    return loudness


def scatter_about(key, extent, scale, reach, shards=(), kind=jnp.bfloat16):
    result = jax.random.normal(key, extent, jnp.float32) * scale
    if len(shards) > 0:
        result = shard_levels(key, extent, shards, -0.22, 0.18) * result
    return jnp.clip(result, min=-reach, max=reach).astype(kind)


def setup_inputs(seed: int = 0) -> dict:
    arg_keys = jax.random.split(jax.random.key(seed), 6)
    return {
        "mol_qkv": draw_mol_qkv(jax.random.fold_in(arg_keys[5], 71), 0),
        "pair_list": draw_pair_list(jax.random.fold_in(arg_keys[5], 71), 0),
        "head_proj": scatter_about(arg_keys[2], (HEADS, HD, R), HD ** -0.5, 0.5, ((0, 4),)),
        "head_out": scatter_about(arg_keys[3], (HEADS, R), R ** -0.5, 0.375, ((0, 4),), jnp.float32),
        "labels": touch_ends((jax.random.randint(arg_keys[4], (PAIRS,), 0, 2) < 1).astype(jnp.int32), jax.random.fold_in(arg_keys[4], 1), 0, 1),
    }


loss_scale = 8192.0


def split_heads(rows_in, component, heads, head_dim):
    return rows_in[:, :, component].reshape(rows_in.shape[0], rows_in.shape[1], heads, head_dim)


def forward(query_rows, key_rows, value_rows, head_proj, head_out, inv_root, length):
    scores = jnp.einsum("plhd,pmhd->phlm", query_rows.astype(jnp.float32), key_rows.astype(jnp.float32)) * inv_root
    row_max = jnp.max(scores, axis=-1, keepdims=True)
    lifted = jnp.exp(scores - row_max)
    attn_weights = lifted / jnp.sum(lifted, axis=-1, keepdims=True)
    weights_bf = attn_weights.astype(jnp.bfloat16)
    context = jnp.einsum("phlm,pmhd->plhd", weights_bf.astype(jnp.float32), value_rows.astype(jnp.float32)).astype(jnp.bfloat16)
    hidden = jnp.einsum("plhd,hdr->plhr", context.astype(jnp.float32), head_proj.astype(jnp.float32))
    partial_value = jnp.sum(jax.nn.silu(hidden) * head_out[None, None], axis=(1, 2, 3)) / length
    return partial_value, (attn_weights, weights_bf, hidden)


def backward(query_rows, key_rows, value_rows, head_proj, head_out, saved, grad_out, inv_root, length):
    attn_weights, weights_bf, hidden = saved
    sigmoid_h = jax.nn.sigmoid(hidden)
    silu_slope = sigmoid_h * (1.0 + hidden * (1.0 - sigmoid_h))
    dhidden = (grad_out[:, None, None, None] / length * head_out[None, None] * silu_slope).astype(jnp.bfloat16)
    dcontext = jnp.einsum("plhr,hdr->plhd", dhidden.astype(jnp.float32), head_proj.astype(jnp.float32)).astype(jnp.bfloat16)
    dvalues = jnp.einsum("phlm,plhd->pmhd", weights_bf.astype(jnp.float32), dcontext.astype(jnp.float32))
    dweights = jnp.einsum("plhd,pmhd->phlm", dcontext.astype(jnp.float32), value_rows.astype(jnp.float32))
    dscores = (attn_weights * (dweights - jnp.sum(dweights * attn_weights, axis=-1, keepdims=True)) * inv_root).astype(jnp.bfloat16)
    dqueries = jnp.einsum("phlm,pmhd->plhd", dscores.astype(jnp.float32), key_rows.astype(jnp.float32))
    dkey_rows = jnp.einsum("phlm,plhd->pmhd", dscores.astype(jnp.float32), query_rows.astype(jnp.float32))
    return dqueries, dkey_rows, dvalues


def reference(mol_qkv, pair_list, head_proj, head_out, labels):
    inv_root = HD ** -0.5
    owners = PAIRS // PAIR_DEV
    blocks = pair_list.reshape(owners, PAIR_DEV, 3)
    block_labels_all = labels.reshape(owners, PAIR_DEV)
    position = jnp.arange(PAIR_DEV, dtype=jnp.int32)

    def per_block(accum, inputs):
        block_rows, block_labels, owner = inputs
        first_mol = (owner * MOL_DEV + block_rows[:, 0]).astype(jnp.int32)
        second_mol = (block_rows[:, 1] * MOL_DEV + block_rows[:, 2]).astype(jnp.int32)
        own_rows = mol_qkv[first_mol]
        partner_rows = mol_qkv[second_mol]
        qa, ka, va = [split_heads(own_rows, c, HEADS, HD) for c in range(3)]
        qb, kb, vb = [split_heads(partner_rows, c, HEADS, HD) for c in range(3)]
        part_ab, saved_ab = forward(qa, kb, vb, head_proj, head_out, inv_root, L)
        part_ba, saved_ba = forward(qb, ka, va, head_proj, head_out, inv_root, L)
        logits = part_ab + part_ba
        targets = block_labels.astype(jnp.float32)
        loss_terms = jax.nn.softplus(logits) - targets * logits
        grad_out = (jax.nn.sigmoid(logits) - targets) * loss_scale
        dq_a, dk_b, dv_b = backward(qa, kb, vb, head_proj, head_out, saved_ab, grad_out, inv_root, L)
        dq_b, dk_a, dv_a = backward(qb, ka, va, head_proj, head_out, saved_ba, grad_out, inv_root, L)
        grad_first = jnp.stack([dq_a, dk_a, dv_a], axis=2).reshape(PAIR_DEV, L, 3, HEADS * HD)
        grad_second = jnp.stack([dq_b, dk_b, dv_b], axis=2).reshape(PAIR_DEV, L, 3, HEADS * HD)
        matches = second_mol[:, None] == second_mol[None, :]
        earlier = matches & (position[None, :] < position[:, None])
        leading = jnp.logical_not(jnp.any(earlier, axis=1))
        key_sums = jnp.einsum("pq,qlcz->plcz", matches.astype(jnp.float32), grad_second, precision=lax.Precision.HIGHEST)
        rounded = lax.optimization_barrier(key_sums.astype(jnp.bfloat16)).astype(jnp.float32)
        partner_term = jnp.where(leading[:, None, None, None], rounded, jnp.zeros_like(rounded))
        accum = accum.at[first_mol].add(grad_first)
        accum = accum.at[second_mol].add(partner_term)
        return accum, (logits, jnp.sum(loss_terms))

    accum0 = jnp.zeros((MOLS, L, 3, HEADS * HD), jnp.float32)
    accum, (logits_all, loss_sums) = lax.scan(per_block, accum0, (blocks, block_labels_all, jnp.arange(owners, dtype=jnp.int32)))
    return accum.astype(jnp.bfloat16), logits_all.reshape(PAIRS), jnp.sum(loss_sums) / PAIRS
```

```python
import functools

import jax
import jax.numpy as jnp
from jax import lax
from jax.experimental import pallas as pl
from jax.experimental.pallas import tpu as pltpu
from jax.sharding import PartitionSpec as P

loss_scale = 8192.0
chunks = 2
row_block = 16

NN = (((1,), (0,)), ((), ()))
NT = (((1,), (1,)), ((), ()))
TN = (((0,), (0,)), ((), ()))


def mm(a, b, dims):
    return lax.dot_general(a, b, dims, preferred_element_type=jnp.float32)


def unit_kernel(
    head_dim,
    x_ref,
    y_ref,
    n_ref,
    q_ref,
    k_ref,
    v_ref,
    proj_ref,
    out_ref,
    part_ref,
    dq_ref,
    dk_ref,
    dv_ref,
):
    inv_root = head_dim ** (-0.5)
    heads, _, inner = proj_ref.shape
    length = q_ref.shape[1]

    @pl.when(pl.program_id(0) < n_ref[0])
    def _():
        total = jnp.zeros((8, inner), jnp.float32)
        for h in range(heads):
            cols = slice(h * head_dim, (h + 1) * head_dim)
            q = q_ref[0, :, cols]
            k = k_ref[0, :, cols]
            v = v_ref[0, :, cols]
            proj = proj_ref[h]
            readout = out_ref[h : h + 1, :]
            scores = mm(q, k, NT) * inv_root
            lifted = jnp.exp(scores - jnp.max(scores, axis=-1, keepdims=True))
            weights = lifted * (1.0 / jnp.sum(lifted, axis=-1, keepdims=True))
            weights_bf = weights.astype(jnp.bfloat16)
            context = mm(weights_bf, v, NN).astype(jnp.bfloat16)
            hidden = mm(context, proj, NN)
            sig = 0.5 * jnp.tanh(0.5 * hidden) + 0.5
            silu = hidden * sig
            total += jnp.sum((silu * readout).reshape(length // 8, 8, inner), axis=0)
            dhidden = (readout * (sig + silu * (1.0 - sig))).astype(jnp.bfloat16)
            dcontext = mm(dhidden, proj, NT).astype(jnp.bfloat16)
            dv_ref[0, :, cols] = mm(weights_bf, dcontext, TN).astype(jnp.bfloat16)
            dweights = mm(dcontext, v, NT)
            inner_sum = jnp.sum(dweights * weights, axis=-1, keepdims=True)
            dscores = (weights * (dweights - inner_sum) * inv_root).astype(jnp.bfloat16)
            dq_ref[0, :, cols] = mm(dscores, k, NN).astype(jnp.bfloat16)
            dk_ref[0, :, cols] = mm(dscores, q, TN).astype(jnp.bfloat16)
        part_ref[0] = total


def run_units(unit_x, unit_y, count, q_all, k, v, head_proj, head_out):
    units = unit_x.shape[0]
    heads, head_dim, inner = head_proj.shape
    _, length, width = k.shape

    def out_map(u, x, y, n):
        return (jnp.minimum(u, n[0] - 1), 0, 0)

    rows = jax.ShapeDtypeStruct((units, length, width), jnp.bfloat16)
    row_spec = pl.BlockSpec((1, length, width), out_map)
    return pl.pallas_call(
        functools.partial(unit_kernel, head_dim),
        grid_spec=pltpu.PrefetchScalarGridSpec(
            num_scalar_prefetch=3,
            grid=(units,),
            in_specs=[
                pl.BlockSpec((1, length, width), lambda u, x, y, n: (x[u], 0, 0)),
                pl.BlockSpec((1, length, width), lambda u, x, y, n: (y[u], 0, 0)),
                pl.BlockSpec((1, length, width), lambda u, x, y, n: (y[u], 0, 0)),
                pl.BlockSpec((heads, head_dim, inner), lambda u, x, y, n: (0, 0, 0)),
                pl.BlockSpec((heads, inner), lambda u, x, y, n: (0, 0)),
            ],
            out_specs=[pl.BlockSpec((1, 8, inner), out_map), row_spec, row_spec, row_spec],
        ),
        out_shape=[jax.ShapeDtypeStruct((units, 8, inner), jnp.float32), rows, rows, rows],
        compiler_params=pltpu.CompilerParams(
            dimension_semantics=("arbitrary",), vmem_limit_bytes=32 * 1024 * 1024
        ),
        cost_estimate=pl.CostEstimate(
            flops=20 * units * heads * length * length * head_dim,
            bytes_accessed=12 * units * length * width,
            transcendentals=units * heads * length * (length + inner),
        ),
    )(unit_x, unit_y, count, q_all, k, v, head_proj, head_out)


def sum_kernel(
    x_ref, y_ref, n_ref, g_ref, dq_ref, dk_ref, dv_ref, oq_ref, ok_ref, ov_ref, sq, sk, sv
):
    sq[...] = jnp.zeros_like(sq)
    sk[...] = jnp.zeros_like(sk)
    sv[...] = jnp.zeros_like(sv)

    def step(u, carry):
        x = x_ref[u]
        y = y_ref[u]
        g = g_ref[u]
        sq[x] += g * dq_ref[u].astype(jnp.float32)
        sk[y] += g * dk_ref[u].astype(jnp.float32)
        sv[y] += g * dv_ref[u].astype(jnp.float32)
        return carry

    lax.fori_loop(0, n_ref[0], step, 0)
    oq_ref[...] = sq[...].astype(jnp.bfloat16)
    ok_ref[...] = sk[...].astype(jnp.bfloat16)
    ov_ref[...] = sv[...].astype(jnp.bfloat16)


def run_sums(unit_x, unit_y, count, scale, dq, dk, dv, mols_all, mols_here):
    units, length, width = dq.shape
    in_spec = pl.BlockSpec((units, row_block, width), lambda i, x, y, n, g: (0, i, 0))
    all_spec = pl.BlockSpec((mols_all, row_block, width), lambda i, x, y, n, g: (0, i, 0))
    here_spec = pl.BlockSpec((mols_here, row_block, width), lambda i, x, y, n, g: (0, i, 0))
    here = jax.ShapeDtypeStruct((mols_here, length, width), jnp.bfloat16)
    return pl.pallas_call(
        sum_kernel,
        grid_spec=pltpu.PrefetchScalarGridSpec(
            num_scalar_prefetch=4,
            grid=(length // row_block,),
            in_specs=[in_spec] * 3,
            out_specs=[all_spec, here_spec, here_spec],
            scratch_shapes=[
                pltpu.VMEM((mols_all, row_block, width), jnp.float32),
                pltpu.VMEM((mols_here, row_block, width), jnp.float32),
                pltpu.VMEM((mols_here, row_block, width), jnp.float32),
            ],
        ),
        out_shape=[jax.ShapeDtypeStruct((mols_all, length, width), jnp.bfloat16), here, here],
        compiler_params=pltpu.CompilerParams(
            dimension_semantics=("arbitrary",), vmem_limit_bytes=40 * 1024 * 1024
        ),
        cost_estimate=pl.CostEstimate(
            flops=6 * units * length * width,
            bytes_accessed=2 * (3 * units + mols_all + 2 * mols_here) * length * width,
            transcendentals=0,
        ),
    )(unit_x, unit_y, count, scale, dq, dk, dv)


def local(mol_qkv, pair_list, head_proj, head_out, labels):
    groups = lax.axis_size("group")
    device = lax.axis_index("group")
    mols_here, length, _, row_width = mol_qkv.shape
    heads_here, head_dim, _ = head_proj.shape
    total_pairs = pair_list.shape[0]
    per_owner = total_pairs // groups
    mols_all = mols_here * groups
    held = groups * (2 * per_owner // groups)
    width = row_width // chunks
    heads_each = heads_here // chunks

    pairs = jnp.arange(total_pairs, dtype=jnp.int32)
    owner = pairs // per_owner
    first_all = owner * mols_here + pair_list[:, 0]
    second_all = pair_list[:, 1] * mols_here + pair_list[:, 2]
    own_pair = device * per_owner + jnp.arange(per_owner, dtype=jnp.int32)
    own_x = lax.dynamic_slice_in_dim(second_all, device * per_owner, per_owner)
    own_y = lax.dynamic_slice_in_dim(pair_list[:, 0], device * per_owner, per_owner)
    here = pair_list[:, 1] == device
    rank = jnp.cumsum(here.astype(jnp.int32)) - 1
    slots = jnp.arange(held, dtype=jnp.int32)
    pick = (here[None, :] & (rank[None, :] == slots[:, None])).astype(jnp.int32)
    held_x = jnp.sum(pick * first_all[None, :], axis=1)
    held_y = jnp.sum(pick * pair_list[:, 2][None, :], axis=1)
    held_pair = jnp.sum(pick * pairs[None, :], axis=1)
    unit_x = jnp.concatenate([own_x, held_x]).astype(jnp.int32)
    unit_y = jnp.concatenate([own_y, held_y]).astype(jnp.int32)
    unit_pair = jnp.concatenate([own_pair, held_pair])
    active = per_owner + jnp.sum(here.astype(jnp.int32))
    count = active.reshape(1).astype(jnp.int32)
    valid = jnp.arange(per_owner + held, dtype=jnp.int32) < active
    at_pair = (unit_pair[:, None] == pairs[None, :]) & valid[:, None]

    results = []
    part = 0.0
    for c in range(chunks):
        cols = slice(c * width, (c + 1) * width)
        hs = slice(c * heads_each, (c + 1) * heads_each)
        q_all = lax.all_gather(mol_qkv[:, :, 0, cols], "group", axis=0, tiled=True)
        k = mol_qkv[:, :, 1, cols]
        v = mol_qkv[:, :, 2, cols]
        sums, dq, dk, dv = run_units(
            unit_x, unit_y, count, q_all, k, v, head_proj[hs], head_out[hs]
        )
        part = part + jnp.sum(sums, axis=(1, 2))
        results.append((dq, dk, dv))

    terms = jnp.sum(jnp.where(at_pair, part[:, None], 0.0), axis=0) / length
    first_copy = (lax.axis_index("fsdp") == 0).astype(jnp.float32)
    spread = lax.dynamic_update_slice_in_dim(
        jnp.zeros((total_pairs,), jnp.float32),
        labels.astype(jnp.float32) * first_copy,
        device * per_owner,
        0,
    )
    both = lax.psum(jnp.stack([terms, spread]), ("group", "fsdp"))
    logits, targets = both[0], both[1]
    mean_loss = jnp.sum(jax.nn.softplus(logits) - targets * logits) / total_pairs
    grad_out = (jax.nn.sigmoid(logits) - targets) * loss_scale
    scale = jnp.sum(jnp.where(at_pair, grad_out[None, :], 0.0), axis=1) / length

    dqs, dks, dvs = [], [], []
    for dq, dk, dv in results:
        sq, sk, sv = run_sums(
            unit_x, unit_y, count, scale, dq, dk, dv, mols_all, mols_here
        )
        dqs.append(lax.psum_scatter(sq, "group", scatter_dimension=0, tiled=True))
        dks.append(sk)
        dvs.append(sv)
    mol_grad = jnp.stack(
        [jnp.concatenate(d, axis=-1) for d in (dqs, dks, dvs)], axis=2
    )
    own_logits = lax.dynamic_slice_in_dim(logits, device * per_owner, per_owner)
    return (mol_grad, own_logits, mean_loss)


def solution(mesh):
    placed = (
        P("group", None, None, "fsdp"),
        P(),
        P("fsdp", None, None),
        P("fsdp", None),
        P("group"),
    )
    return jax.shard_map(
        local,
        mesh=mesh,
        in_specs=placed,
        out_specs=(P("group", None, None, "fsdp"), P("group"), P()),
        check_vma=False,
    )
```

```python
import functools

import jax
import jax.numpy as jnp
from jax import lax
from jax.experimental import pallas as pl
from jax.experimental.pallas import tpu as pltpu
from jax.sharding import PartitionSpec as P

loss_scale = 8192.0
most_chunks = 4
row_block = 16

NN = (((1,), (0,)), ((), ()))
NT = (((1,), (1,)), ((), ()))
TN = (((0,), (0,)), ((), ()))


def mm(a, b, dims):
    return lax.dot_general(a, b, dims, preferred_element_type=jnp.float32)


def unit_kernel(
    head_dim,
    x_ref,
    y_ref,
    n_ref,
    q_ref,
    k_ref,
    v_ref,
    proj_ref,
    out_ref,
    part_ref,
    dq_ref,
    dk_ref,
    dv_ref,
):
    inv_root = head_dim ** (-0.5)
    heads, _, inner = proj_ref.shape
    length = q_ref.shape[1]

    @pl.when(pl.program_id(0) < n_ref[0])
    def _():
        total = jnp.zeros((8, inner), jnp.float32)
        for h in range(heads):
            cols = slice(h * head_dim, (h + 1) * head_dim)
            q = q_ref[0, :, cols]
            k = k_ref[0, :, cols]
            v = v_ref[0, :, cols]
            proj = proj_ref[h]
            readout = out_ref[h : h + 1, :]
            scores = mm(q, k, NT) * inv_root
            lifted = jnp.exp(scores - jnp.max(scores, axis=-1, keepdims=True))
            weights = lifted * (1.0 / jnp.sum(lifted, axis=-1, keepdims=True))
            weights_bf = weights.astype(jnp.bfloat16)
            context = mm(weights_bf, v, NN).astype(jnp.bfloat16)
            hidden = mm(context, proj, NN)
            sig = 0.5 * jnp.tanh(0.5 * hidden) + 0.5
            silu = hidden * sig
            total += jnp.sum((silu * readout).reshape(length // 8, 8, inner), axis=0)
            dhidden = (readout * (sig + silu * (1.0 - sig))).astype(jnp.bfloat16)
            dcontext = mm(dhidden, proj, NT).astype(jnp.bfloat16)
            dv_ref[0, :, cols] = mm(weights_bf, dcontext, TN).astype(jnp.bfloat16)
            dweights = mm(dcontext, v, NT)
            inner_sum = jnp.sum(dweights * weights, axis=-1, keepdims=True)
            dscores = (weights * (dweights - inner_sum) * inv_root).astype(jnp.bfloat16)
            dq_ref[0, :, cols] = mm(dscores, k, NN).astype(jnp.bfloat16)
            dk_ref[0, :, cols] = mm(dscores, q, TN).astype(jnp.bfloat16)
        part_ref[0] = total


def run_units(unit_x, unit_y, count, q_all, k, v, head_proj, head_out):
    units = unit_x.shape[0]
    heads, head_dim, inner = head_proj.shape
    _, length, width = k.shape

    def out_map(u, x, y, n):
        return (jnp.minimum(u, n[0] - 1), 0, 0)

    rows = jax.ShapeDtypeStruct((units, length, width), jnp.bfloat16)
    row_spec = pl.BlockSpec((1, length, width), out_map)
    return pl.pallas_call(
        functools.partial(unit_kernel, head_dim),
        grid_spec=pltpu.PrefetchScalarGridSpec(
            num_scalar_prefetch=3,
            grid=(units,),
            in_specs=[
                pl.BlockSpec((1, length, width), lambda u, x, y, n: (x[u], 0, 0)),
                pl.BlockSpec((1, length, width), lambda u, x, y, n: (y[u], 0, 0)),
                pl.BlockSpec((1, length, width), lambda u, x, y, n: (y[u], 0, 0)),
                pl.BlockSpec((heads, head_dim, inner), lambda u, x, y, n: (0, 0, 0)),
                pl.BlockSpec((heads, inner), lambda u, x, y, n: (0, 0)),
            ],
            out_specs=[pl.BlockSpec((1, 8, inner), out_map), row_spec, row_spec, row_spec],
        ),
        out_shape=[jax.ShapeDtypeStruct((units, 8, inner), jnp.float32), rows, rows, rows],
        compiler_params=pltpu.CompilerParams(
            dimension_semantics=("arbitrary",), vmem_limit_bytes=60 * 1024 * 1024
        ),
        cost_estimate=pl.CostEstimate(
            flops=20 * units * heads * length * length * head_dim,
            bytes_accessed=12 * units * length * width,
            transcendentals=units * heads * length * (length + inner),
        ),
    )(unit_x, unit_y, count, q_all, k, v, head_proj, head_out)


def sum_kernel(
    x_ref, y_ref, n_ref, g_ref, dq_ref, dk_ref, dv_ref, oq_ref, ok_ref, ov_ref, sq, sk, sv
):
    sq[...] = jnp.zeros_like(sq)
    sk[...] = jnp.zeros_like(sk)
    sv[...] = jnp.zeros_like(sv)

    def step(u, carry):
        x = x_ref[u]
        y = y_ref[u]
        g = g_ref[u]
        sq[x] += g * dq_ref[u].astype(jnp.float32)
        sk[y] += g * dk_ref[u].astype(jnp.float32)
        sv[y] += g * dv_ref[u].astype(jnp.float32)
        return carry

    lax.fori_loop(0, n_ref[0], step, 0)
    oq_ref[...] = sq[...].astype(jnp.bfloat16)
    ok_ref[...] = sk[...].astype(jnp.bfloat16)
    ov_ref[...] = sv[...].astype(jnp.bfloat16)


def run_sums(unit_x, unit_y, count, scale, dq, dk, dv, mols_all, mols_here):
    units, length, width = dq.shape
    in_spec = pl.BlockSpec((units, row_block, width), lambda i, x, y, n, g: (0, i, 0))
    all_spec = pl.BlockSpec((mols_all, row_block, width), lambda i, x, y, n, g: (0, i, 0))
    here_spec = pl.BlockSpec((mols_here, row_block, width), lambda i, x, y, n, g: (0, i, 0))
    here = jax.ShapeDtypeStruct((mols_here, length, width), jnp.bfloat16)
    return pl.pallas_call(
        sum_kernel,
        grid_spec=pltpu.PrefetchScalarGridSpec(
            num_scalar_prefetch=4,
            grid=(length // row_block,),
            in_specs=[in_spec] * 3,
            out_specs=[all_spec, here_spec, here_spec],
            scratch_shapes=[
                pltpu.VMEM((mols_all, row_block, width), jnp.float32),
                pltpu.VMEM((mols_here, row_block, width), jnp.float32),
                pltpu.VMEM((mols_here, row_block, width), jnp.float32),
            ],
        ),
        out_shape=[jax.ShapeDtypeStruct((mols_all, length, width), jnp.bfloat16), here, here],
        compiler_params=pltpu.CompilerParams(
            dimension_semantics=("arbitrary",), vmem_limit_bytes=60 * 1024 * 1024
        ),
        cost_estimate=pl.CostEstimate(
            flops=6 * units * length * width,
            bytes_accessed=2 * (3 * units + mols_all + 2 * mols_here) * length * width,
            transcendentals=0,
        ),
    )(unit_x, unit_y, count, scale, dq, dk, dv)


def local(mol_qkv, pair_list, head_proj, head_out, labels):
    groups = lax.axis_size("group")
    device = lax.axis_index("group")
    mols_here, length, _, row_width = mol_qkv.shape
    heads_here, head_dim, _ = head_proj.shape
    total_pairs = pair_list.shape[0]
    per_owner = total_pairs // groups
    mols_all = mols_here * groups
    held = groups * (2 * per_owner // groups)
    chunks = min(most_chunks, heads_here)
    width = row_width // chunks
    heads_each = heads_here // chunks

    pairs = jnp.arange(total_pairs, dtype=jnp.int32)
    owner = pairs // per_owner
    first_all = owner * mols_here + pair_list[:, 0]
    second_all = pair_list[:, 1] * mols_here + pair_list[:, 2]
    own_pair = device * per_owner + jnp.arange(per_owner, dtype=jnp.int32)
    own_x = lax.dynamic_slice_in_dim(second_all, device * per_owner, per_owner)
    own_y = lax.dynamic_slice_in_dim(pair_list[:, 0], device * per_owner, per_owner)
    here = pair_list[:, 1] == device
    rank = jnp.cumsum(here.astype(jnp.int32)) - 1
    slots = jnp.arange(held, dtype=jnp.int32)
    pick = (here[None, :] & (rank[None, :] == slots[:, None])).astype(jnp.int32)
    held_x = jnp.sum(pick * first_all[None, :], axis=1)
    held_y = jnp.sum(pick * pair_list[:, 2][None, :], axis=1)
    held_pair = jnp.sum(pick * pairs[None, :], axis=1)
    unit_x = jnp.concatenate([own_x, held_x]).astype(jnp.int32)
    unit_y = jnp.concatenate([own_y, held_y]).astype(jnp.int32)
    unit_pair = jnp.concatenate([own_pair, held_pair])
    active = per_owner + jnp.sum(here.astype(jnp.int32))
    count = active.reshape(1).astype(jnp.int32)
    valid = jnp.arange(per_owner + held, dtype=jnp.int32) < active
    at_pair = (unit_pair[:, None] == pairs[None, :]) & valid[:, None]

    results = []
    part = 0.0
    for c in range(chunks):
        cols = slice(c * width, (c + 1) * width)
        hs = slice(c * heads_each, (c + 1) * heads_each)
        q_all = lax.all_gather(mol_qkv[:, :, 0, cols], "group", axis=0, tiled=True)
        k = mol_qkv[:, :, 1, cols]
        v = mol_qkv[:, :, 2, cols]
        sums, dq, dk, dv = run_units(
            unit_x, unit_y, count, q_all, k, v, head_proj[hs], head_out[hs]
        )
        part = part + jnp.sum(sums, axis=(1, 2))
        results.append((dq, dk, dv))

    terms = jnp.sum(jnp.where(at_pair, part[:, None], 0.0), axis=0) / length
    first_copy = (lax.axis_index("fsdp") == 0).astype(jnp.float32)
    spread = lax.dynamic_update_slice_in_dim(
        jnp.zeros((total_pairs,), jnp.float32),
        labels.astype(jnp.float32) * first_copy,
        device * per_owner,
        0,
    )
    shares = lax.all_gather(jnp.stack([terms, spread]), ("group", "fsdp"), axis=0)
    both = jnp.sum(shares, axis=0)
    logits, targets = both[0], both[1]
    mean_loss = jnp.sum(jax.nn.softplus(logits) - targets * logits) / total_pairs
    grad_out = (jax.nn.sigmoid(logits) - targets) * loss_scale
    scale = jnp.sum(jnp.where(at_pair, grad_out[None, :], 0.0), axis=1) / length

    dqs, dks, dvs = [], [], []
    for dq, dk, dv in results:
        sq, sk, sv = run_sums(
            unit_x, unit_y, count, scale, dq, dk, dv, mols_all, mols_here
        )
        dqs.append(lax.psum_scatter(sq, "group", scatter_dimension=0, tiled=True))
        dks.append(sk)
        dvs.append(sv)
    mol_grad = jnp.stack(
        [jnp.concatenate(d, axis=-1) for d in (dqs, dks, dvs)], axis=2
    )
    own_logits = lax.dynamic_slice_in_dim(logits, device * per_owner, per_owner)
    return (mol_grad, own_logits, mean_loss)


def solution(mesh):
    placed = (
        P("group", None, None, "fsdp"),
        P(),
        P("fsdp", None, None),
        P("fsdp", None),
        P("group"),
    )
    return jax.shard_map(
        local,
        mesh=mesh,
        in_specs=placed,
        out_specs=(P("group", None, None, "fsdp"), P("group"), P()),
        check_vma=False,
    )
```
